256 devices in a mesh: tile: 32 (over x_hi, z, core), wave: 8 (over x_lo, y).
Axes of the slice: x: 4 (x_hi: 2, x_lo: 2; x = x_hi * 2 + x_lo), y: 4, z: 8, core: 2. Of those that a mesh axis runs over, the one named last changes fastest.
Arguments:
- params: float32 [9, 512, 128], P(None, 'tile'), may hold values from -6 to 6
- dual_in: float32 [2, 9, 512, 128], P(None, None, 'tile'), may hold values from -4 to 4
- jacobian: bfloat16 [4, 9, 512, 128], P(None, None, 'tile'), may hold values from -3 to 3
- response: float32 [9, 256], P(None, 'wave'), may hold values from -5 to 5
- observed: bfloat16 [4, 256, 512, 128], P(None, 'wave', 'tile'), may hold values from -6 to 6
- psf: bfloat16 [17, 17], replicated, may hold values from -0.375 to 0.375
- step_size: float32 [], replicated, may hold values from 0.03 to 0.06
- dual_step: float32 [], replicated, may hold values from 0.5 to 1
- tv_bound: float32 [], replicated, may hold values from 1 to 2
- clip_bound: float32 [], replicated, may hold values from 0.5 to 1
Outputs:
- params_out: float32 [9, 512, 128], P(None, 'tile')
- dual_out: float32 [2, 9, 512, 128], P(None, None, 'tile')
- misfit: float32 [], replicated
The draws below stay inside these ranges and needn't reach their ends.
All inputs are finite; a program needn't handle non-finite values.
Results may differ from the reference program's by a relative error of at most 0.0033.
Values may be sent and summed in bfloat16 or wider, within the bound.
No kernel may reach another device: no remote copies, remote signals or barrier semaphores. Data moves between devices by JAX's collectives and lax.ppermute only.
A program may use at most 128 MiB of HBM per device.

```python
import jax
import jax.numpy as jnp
from jax import lax

NCOL = 128
NPAR = 9
STOKES = 4
TAPS = 17
NROWS = 512
WAVE = 256


def block_levels(key, shape, shards, least, high):
    gain = 1.0
    for position, shards_of in shards:
        heights = jax.random.uniform(jax.random.fold_in(jax.random.fold_in(key, 6), position), (shards_of,), jnp.float32, least / len(shards), high / len(shards))
        gain = gain * jnp.repeat(jnp.exp(heights), shape[position] // shards_of).reshape((-1,) + (1,) * (len(shape) - 1 - position))
    return gain


def centred(own_key, dims, width, reach, pieces=(), kind=jnp.bfloat16):
    values = width * jax.random.normal(own_key, dims, jnp.float32)
    if pieces:
        values = values * block_levels(own_key, dims, pieces, -0.22, 0.18)
    return jnp.clip(values, -reach, reach).astype(kind)


def setup_inputs(seed: int = 0) -> dict:
    streams_of = jax.random.split(jax.random.key(seed), 11)
    params = centred(streams_of[0], (NPAR, NROWS, NCOL), 1.0, 6.0, ((1, 32),), jnp.float32)
    dual_in = centred(streams_of[1], (2, NPAR, NROWS, NCOL), 0.5, 4.0, ((2, 32),), jnp.float32)
    jacobian = centred(streams_of[2], (STOKES, NPAR, NROWS, NCOL), 0.35, 3.0, ((2, 32),))
    response = centred(streams_of[3], (NPAR, WAVE), 1.0, 5.0, ((1, 8),), jnp.float32)
    observed = centred(streams_of[4], (STOKES, WAVE, NROWS, NCOL), 1.0, 6.0, ((1, 8), (2, 32)))
    psf = centred(streams_of[5], (TAPS, TAPS), (TAPS * TAPS) ** -0.5, 0.375)
    step_size = jnp.clip(jax.random.uniform(streams_of[6], (), jnp.float32, 0.03, 0.06), 0.03, 0.06)
    dual_step = jnp.clip(jax.random.uniform(streams_of[7], (), jnp.float32, 0.5, 1.0), 0.5, 1.0)
    tv_bound = jnp.clip(jax.random.uniform(streams_of[8], (), jnp.float32, 1.0, 2.0), 1.0, 2.0)
    clip_bound = jnp.clip(jax.random.uniform(streams_of[9], (), jnp.float32, 0.5, 1.0), 0.5, 1.0)
    return dict(params=params, dual_in=dual_in, jacobian=jacobian, response=response, observed=observed, psf=psf, step_size=step_size, dual_step=dual_step, tv_bound=tv_bound, clip_bound=clip_bound)


def toeplitz(psf, ncol):
    rows = jnp.arange(ncol, dtype=jnp.int32)[:, None]
    cols = jnp.arange(ncol, dtype=jnp.int32)[None, :]
    offset = (rows - cols + 8) % ncol
    onehot = (offset[None] == jnp.arange(17, dtype=jnp.int32)[:, None, None]).astype(jnp.float32)
    mats = jnp.einsum('ab,bkj->akj', psf.astype(jnp.float32), onehot, precision=lax.Precision.HIGHEST)
    return mats.astype(jnp.bfloat16)


def blur_rows(padded, mats, adjoint):
    count = padded.shape[1] - 16
    total = jnp.zeros((padded.shape[0], count, padded.shape[2]), jnp.float32)
    for tap in range(17):
        window = padded[:, tap:tap + count].astype(jnp.float32)
        if adjoint:
            total = total + jnp.einsum('nrk,jk->nrj', window, mats[16 - tap].astype(jnp.float32), precision=lax.Precision.HIGHEST)
        else:
            total = total + jnp.einsum('nrk,kj->nrj', window, mats[tap].astype(jnp.float32), precision=lax.Precision.HIGHEST)
    return total


def wrap_rows(image):
    return jnp.concatenate([image[:, -8:], image, image[:, :8]], axis=1)


def reference(params, dual_in, jacobian, response, observed, psf, step_size, dual_step, tv_bound, clip_bound):
    mats = toeplitz(psf, params.shape[2])
    grad_r = jnp.roll(params, -1, axis=1) - params
    grad_c = jnp.roll(params, -1, axis=2) - params
    dual_out = jnp.clip(dual_in + dual_step * jnp.stack([grad_r, grad_c]), -tv_bound, tv_bound)
    divergence = (dual_out[0] - jnp.roll(dual_out[0], 1, axis=1)) + (dual_out[1] - jnp.roll(dual_out[1], 1, axis=2))

    def gradient(state):
        def per_stokes(pair):
            jac_one, obs_one = pair
            terms = jac_one.astype(jnp.float32) * state
            synthetic = jnp.einsum('pl,pij->lij', response, terms, precision=lax.Precision.HIGHEST).astype(jnp.bfloat16)
            blurred = blur_rows(wrap_rows(synthetic), mats, False)
            resid = blurred - obs_one.astype(jnp.float32)
            size = jnp.abs(resid)
            huber = jnp.sum(jnp.where(size <= clip_bound, 0.5 * resid * resid, clip_bound * size - 0.5 * clip_bound * clip_bound))
            weighted = jnp.clip(resid, -clip_bound, clip_bound).astype(jnp.bfloat16)
            back = blur_rows(wrap_rows(weighted), mats, True)
            along = jnp.einsum('pl,lij->pij', response, back, precision=lax.Precision.HIGHEST)
            return jac_one.astype(jnp.float32) * along, huber

        parts, hubers = lax.map(per_stokes, (jacobian, observed))
        return jnp.sum(parts, axis=0), jnp.sum(hubers)

    state = params
    misfit = jnp.float32(0.0)
    for step in range(2):
        grad_now, huber = gradient(state)
        if step == 0:
            misfit = huber / (observed.shape[0] * observed.shape[1] * observed.shape[2] * observed.shape[3])
        state = state - step_size * (grad_now - divergence)
    return state, dual_out, misfit
```

```python
import functools

import jax
import jax.numpy as jnp
from jax import lax
from jax.experimental import pallas as pl
from jax.experimental.pallas import tpu as pltpu
from jax.sharding import Mesh
from jax.sharding import PartitionSpec as P

TILE = ("tile_0", "tile_1", "tile_2")
WAVE = ("wave_0", "wave_1")
ALL = TILE + WAVE
F32 = jnp.float32
BF16 = jnp.bfloat16

SP = 36
SPP = 40
HL = 2 * SPP
TAPS = 17
PAIRS = 9


def passed_along(x, axis, by):
    devices = lax.axis_size(axis)
    return lax.ppermute(x, axis, [(i, (i + by) % devices) for i in range(devices)])


def split_rows(value):
    high = value.astype(BF16).astype(F32)
    return jnp.concatenate([high, value - high], axis=0).astype(BF16)


def weights_kernel(psf_ref, forward_ref, adjoint_ref):
    n = 128
    row = lax.broadcasted_iota(jnp.int32, (n, n), 0)
    col = lax.broadcasted_iota(jnp.int32, (n, n), 1)
    offset = lax.rem(row - col + (n + 8), n)
    zero = jnp.zeros((n, n), BF16)
    for ref in (forward_ref, adjoint_ref):
        ref[0:n, n : 2 * n] = zero
        ref[TAPS * n : (TAPS + 1) * n, 0:n] = zero
    for tap in range(TAPS):
        for ref, flip in ((forward_ref, False), (adjoint_ref, True)):
            mat = jnp.zeros((n, n), F32)
            for b in range(TAPS):
                scalar = psf_ref[16 - tap, 16 - b] if flip else psf_ref[tap, b]
                mat = jnp.where(offset == b, scalar, mat)
            mat = mat.astype(BF16)
            ref[tap * n : (tap + 1) * n, 0:n] = mat
            ref[(tap + 1) * n : (tap + 2) * n, n : 2 * n] = mat


def step_kernel(
    clip_ref,
    x_lo, x_own, x_hi,
    j_lo, j_own, j_hi,
    o_lo, o_own, o_hi,
    resp_ref, resp_t_ref,
    forward_ref, adjoint_ref,
    out_ref,
    terms, stacked, obs, contracted, along,
):
    n = 128
    clip = clip_ref[0]
    terms[SP * 48 : SPP * 48, :] = jnp.zeros(((SPP - SP) * 48, n), F32)
    for part, (x_ref, j_ref) in enumerate(((x_lo, j_lo), (x_own, j_own), (x_hi, j_hi))):
        for image in range(SP):
            terms[image * 48 + part * 16 : image * 48 + part * 16 + 16, :] = (
                j_ref[image].astype(F32) * x_ref[image % 9]
            )
    obs[:, 0:8, :] = o_lo[...].astype(F32)
    obs[:, 8:24, :] = o_own[...].astype(F32)
    obs[:, 24:32, :] = o_hi[...].astype(F32)
    obs_flat = obs.reshape(128 * 32, n)
    for row in range(48):
        pair, half = row // 2, row % 2
        stacked[pair * HL : (pair + 1) * HL, half * n : (half + 1) * n] = split_rows(
            terms[pl.ds(row, SPP, stride=48), :]
        )
    huber = jnp.zeros((8, 2 * n), F32)
    for block in range(4):
        windows = [
            stacked[(4 * block + k) * HL : (4 * block + k + 4) * HL, :] for k in range(PAIRS)
        ]
        blurred = jnp.dot(
            jnp.concatenate(windows, axis=1), forward_ref[...], preferred_element_type=F32
        )
        for i in range(4):
            pair = 4 * block + i
            model = blurred[i * HL : i * HL + SPP] + blurred[i * HL + SPP : (i + 1) * HL]
            high = model.astype(BF16).astype(F32)
            model = jnp.concatenate(
                [high, model - high, high, jnp.zeros((8, 2 * n), F32)], axis=0
            ).astype(BF16)
            seen = jnp.concatenate(
                [
                    obs_flat[pl.ds(2 * pair, 128, stride=32), :],
                    obs_flat[pl.ds(2 * pair + 1, 128, stride=32), :],
                ],
                axis=1,
            )
            resid = jnp.dot(resp_ref[...], model, preferred_element_type=F32) - seen
            weighted = jnp.clip(resid, -clip, clip)
            if 4 <= pair < 12:
                loss = weighted * (resid - 0.5 * weighted)
                huber = huber + jnp.sum(loss.reshape(16, 8, 2 * n), axis=0)
            summed = jnp.dot(
                resp_t_ref[...], weighted.astype(BF16), preferred_element_type=F32
            )
            contracted[pair * HL : (pair + 1) * HL, :] = split_rows(
                summed[:SPP] + summed[SPP:]
            )
    for block in range(2):
        windows = [
            contracted[(4 * block + k) * HL : (4 * block + k + 4) * HL, :] for k in range(PAIRS)
        ]
        back = jnp.dot(
            jnp.concatenate(windows, axis=1), adjoint_ref[...], preferred_element_type=F32
        )
        for i in range(4):
            pair = 4 * block + i
            both = back[i * HL : i * HL + SPP] + back[i * HL + SPP : (i + 1) * HL]
            along[pl.ds(2 * pair, SPP, stride=16), :] = both[:, :n]
            along[pl.ds(2 * pair + 1, SPP, stride=16), :] = both[:, n:]
    for p in range(9):
        total = jnp.zeros((16, n), F32)
        for s in range(4):
            image = s * 9 + p
            total = total + j_own[image].astype(F32) * along[image * 16 : image * 16 + 16, :]
        for copy in range(8):
            out_ref[copy, p * 16 : p * 16 + 16, :] = total
    for copy in range(8):
        out_ref[copy, 144:152, :] = huber[:, :n] + huber[:, n:]


def vmem_specs(count):
    return [pl.BlockSpec(memory_space=pltpu.VMEM) for _ in range(count)]


def blur_weights(psf):
    shape = jax.ShapeDtypeStruct((18 * 128, 256), BF16)
    return pl.pallas_call(
        weights_kernel,
        out_shape=(shape, shape),
        in_specs=[pl.BlockSpec(memory_space=pltpu.SMEM)],
        out_specs=tuple(vmem_specs(2)),
        name="blur_weights",
    )(psf.astype(F32))


def partial_gradient(clip_bound, x, jac, obs, resp, resp_t, forward, adjoint):
    return pl.pallas_call(
        step_kernel,
        out_shape=jax.ShapeDtypeStruct((8, 152, 128), F32),
        in_specs=[pl.BlockSpec(memory_space=pltpu.SMEM)] + vmem_specs(13),
        out_specs=pl.BlockSpec(memory_space=pltpu.VMEM),
        scratch_shapes=[
            pltpu.VMEM((SPP * 48, 128), F32),
            pltpu.VMEM((24 * HL, 256), BF16),
            pltpu.VMEM((128, 32, 128), F32),
            pltpu.VMEM((16 * HL, 256), BF16),
            pltpu.VMEM((SPP * 16, 128), F32),
        ],
        compiler_params=pltpu.CompilerParams(vmem_limit_bytes=40 * 1024 * 1024),
        cost_estimate=pl.CostEstimate(
            flops=3_000_000_000, bytes_accessed=6_000_000, transcendentals=0
        ),
        name="partial_gradient",
    )(clip_bound.reshape(1), *x, *jac, *obs, resp, resp_t, forward, adjoint)


def response_matrices(response):
    block = jnp.einsum("st,pl->sltp", jnp.eye(4, dtype=F32), response).reshape(128, SP)
    block = jnp.pad(block, ((0, 0), (0, SPP - SP)))
    high = block.astype(BF16).astype(F32)
    low = block - high
    forward = jnp.concatenate([high, high, low, jnp.zeros((128, 8), F32)], axis=1)
    backward = jnp.concatenate([high.T, low.T], axis=0)
    return forward.astype(BF16), backward.astype(BF16)


def per_device(
    params, dual_in, jacobian, response, observed, psf, step_size, dual_step, tv_bound, clip_bound
):
    stokes, waves, rows, ncol = observed.shape
    jac = jacobian.reshape(SP, rows, ncol)
    obs = observed.reshape(stokes * waves, rows, ncol)
    x_lo, x_hi = passed_along(params, TILE, 1), passed_along(params, TILE, -1)
    j_lo, j_hi = passed_along(jac, TILE, 1), passed_along(jac, TILE, -1)
    o_lo = passed_along(obs[:, rows - 8 :], TILE, 1)
    o_hi = passed_along(obs[:, :8], TILE, -1)
    jac = (j_lo, jac, j_hi)
    obs = (o_lo, obs, o_hi)
    forward, adjoint = blur_weights(psf)
    resp, resp_t = response_matrices(response)

    grad_r = jnp.concatenate([params[:, 1:], x_hi[:, :1]], axis=1) - params
    grad_c = jnp.roll(params, -1, axis=2) - params
    dual_out = jnp.clip(dual_in + dual_step * jnp.stack([grad_r, grad_c]), -tv_bound, tv_bound)
    preceding = passed_along(dual_out[0][:, -1:], TILE, 1)
    divergence = dual_out[0] - jnp.concatenate([preceding, dual_out[0][:, :-1]], axis=1)
    divergence = divergence + (dual_out[1] - jnp.roll(dual_out[1], 1, axis=2))

    part = partial_gradient(clip_bound, (x_lo, params, x_hi), jac, obs, resp, resp_t, forward, adjoint)
    whole = lax.all_to_all(part, WAVE, 0, 0, tiled=True).sum(axis=0)
    state = params - step_size * (whole[:144].reshape(9, rows, ncol) - divergence)
    loss = whole[144:]

    x_lo, x_hi = passed_along(state, TILE, 1), passed_along(state, TILE, -1)
    tiles, wavs = lax.axis_size(TILE), lax.axis_size(WAVE)
    each = tiles // wavs
    losses = [
        lax.ppermute(
            loss,
            ALL,
            [
                (((t + each * w + k) % tiles) * wavs + w, t * wavs + w)
                for t in range(tiles)
                for w in range(wavs)
            ],
        )
        for k in range(each)
    ]
    loss = sum(losses[1:], losses[0])
    part = partial_gradient(clip_bound, (x_lo, state, x_hi), jac, obs, resp, resp_t, forward, adjoint)
    part = part.at[:, 144:].set(jnp.broadcast_to(loss, (8, 8, ncol)))
    whole = lax.all_to_all(part, WAVE, 0, 0, tiled=True).sum(axis=0)
    state = state - step_size * (whole[:144].reshape(9, rows, ncol) - divergence)
    total = stokes * waves * wavs * rows * tiles * ncol
    misfit = jnp.sum(whole[144:]) / total
    return (state, dual_out, misfit)


def solution(mesh):
    split = Mesh(
        mesh.devices.reshape(2, 8, 2, 2, 4), ("tile_0", "tile_1", "tile_2", "wave_0", "wave_1")
    )
    placed = (
        P(None, TILE, None),
        P(None, None, TILE, None),
        P(None, None, TILE, None),
        P(None, WAVE),
        P(None, WAVE, TILE, None),
        P(),
        P(),
        P(),
        P(),
        P(),
    )
    return jax.shard_map(
        per_device,
        mesh=split,
        in_specs=placed,
        out_specs=(P(None, TILE, None), P(None, None, TILE, None), P()),
        check_vma=False,
    )
```

```python
import functools

import jax
import jax.numpy as jnp
from jax import lax
from jax.experimental import pallas as pl
from jax.experimental.pallas import tpu as pltpu
from jax.sharding import Mesh
from jax.sharding import PartitionSpec as P

TILE = ("tile_0", "tile_1", "tile_2")
WAVE = ("wave_0", "wave_1")
ALL = TILE + WAVE
F32 = jnp.float32
BF16 = jnp.bfloat16

SP = 36
SPP = 40
HL = 2 * SPP
TAPS = 17
PAIRS = 9
LANES = 128
AT_JAC = 1024
AT_X = AT_JAC + SP * 16
AT_DUAL = AT_X + 3 * 144
HALO = AT_DUAL + 48


def neighbours(tiles, waves, by):
    return [
        (t * waves + w, ((t + by) % tiles) * waves + w) for t in range(tiles) for w in range(waves)
    ]


def passed_along(x, by):
    return lax.ppermute(x, ALL, neighbours(lax.axis_size(TILE), lax.axis_size(WAVE), by))


def rounded(value):
    return value.astype(BF16).astype(F32)


def split_rows(value):
    high = rounded(value)
    return jnp.concatenate([high, value - high], axis=0).astype(BF16)


def thirds(value):
    high = rounded(value)
    mid = rounded(value - high)
    return high, mid, value - high - mid


def halo_kernel(x_ref, dual_ref, jac_ref, obs_ref, up_ref, down_ref):
    dual = jnp.concatenate([dual_ref[0, :, 15, :], jnp.zeros((7, LANES), F32)], axis=0)
    duals = thirds(dual)
    for ref, first in ((up_ref, 8), (down_ref, 0)):
        ref[0:AT_JAC, :] = obs_ref[:, first : first + 8, :].reshape(AT_JAC, LANES)
        ref[AT_JAC:AT_X, :] = jac_ref[...].reshape(SP * 16, LANES)
        for i in range(3):
            ref[AT_DUAL + 16 * i : AT_DUAL + 16 * i + 16, :] = duals[i].astype(BF16)
    for p in range(9):
        for i, part in enumerate(thirds(x_ref[p])):
            at = AT_X + 144 * i + 16 * p
            up_ref[at : at + 16, :] = part.astype(BF16)
            down_ref[at : at + 16, :] = part.astype(BF16)


def halo_x(ref, p):
    return sum(ref[AT_X + 144 * i + 16 * p : AT_X + 144 * i + 16 * p + 16, :].astype(F32) for i in range(3))


def weights_kernel(psf_ref, obs_ref, forward_ref, adjoint_ref, seen_ref, rows_ref):
    n = LANES
    row = lax.broadcasted_iota(jnp.int32, (n, n), 0)
    col = lax.broadcasted_iota(jnp.int32, (n, n), 1)
    offset = lax.rem(row - col + (n + 8), n)
    zero = jnp.zeros((n, n), BF16)
    for ref in (forward_ref, adjoint_ref):
        ref[0:n, n : 2 * n] = zero
        ref[TAPS * n : (TAPS + 1) * n, 0:n] = zero
    for tap in range(TAPS):
        for ref, flip in ((forward_ref, False), (adjoint_ref, True)):
            mat = jnp.zeros((n, n), F32)
            for b in range(TAPS):
                scalar = psf_ref[16 - tap, 16 - b] if flip else psf_ref[tap, b]
                mat = jnp.where(offset == b, scalar, mat)
            mat = mat.astype(BF16)
            ref[tap * n : (tap + 1) * n, 0:n] = mat
            ref[(tap + 1) * n : (tap + 2) * n, n : 2 * n] = mat
    rows_ref[...] = obs_ref[...].astype(F32).reshape(128 * 16, n)
    for r in range(16):
        seen_ref[:, r * n : (r + 1) * n] = rows_ref[pl.ds(r, 128, stride=16), :]


def step_kernel(
    first,
    clip_ref,
    lo_ref, hi_ref, x_lo, x_own, x_hi, jac_ref, seen_ref,
    resp_ref, resp_t_ref, forward_ref, adjoint_ref,
    out_ref,
    terms, stacked, halo, contracted, along,
):
    n = LANES
    clip = clip_ref[0]
    terms[SP * 48 : SPP * 48, :] = jnp.zeros(((SPP - SP) * 48, n), F32)
    for part, (x_ref, ref) in enumerate(((x_lo, lo_ref), (x_own, None), (x_hi, hi_ref))):
        for p in range(9):
            if first and ref is not None:
                x = halo_x(ref, p)
            else:
                x = x_ref[p * 16 : p * 16 + 16, :]
            for s in range(4):
                image = s * 9 + p
                if ref is None:
                    jac = jac_ref[image]
                else:
                    jac = ref[AT_JAC + image * 16 : AT_JAC + image * 16 + 16, :]
                terms[image * 48 + part * 16 : image * 48 + part * 16 + 16, :] = (
                    jac.astype(F32) * x
                )
    halo[0:AT_JAC, :] = lo_ref[0:AT_JAC, :].astype(F32)
    halo[AT_JAC : 2 * AT_JAC, :] = hi_ref[0:AT_JAC, :].astype(F32)
    for row in range(48):
        pair, half = row // 2, row % 2
        stacked[pair * HL : (pair + 1) * HL, half * n : (half + 1) * n] = split_rows(
            terms[pl.ds(row, SPP, stride=48), :]
        )
    huber = jnp.zeros((8, 8 * n), F32)
    for block in range(4):
        windows = [
            stacked[(4 * block + k) * HL : (4 * block + k + 4) * HL, :] for k in range(PAIRS)
        ]
        blurred = jnp.dot(
            jnp.concatenate(windows, axis=1), forward_ref[...], preferred_element_type=F32
        )
        model = jnp.concatenate(
            [
                blurred[i * HL : i * HL + SPP] + blurred[i * HL + SPP : (i + 1) * HL]
                for i in range(4)
            ],
            axis=1,
        )
        high = rounded(model)
        model = jnp.concatenate(
            [high, model - high, high, jnp.zeros((8, 8 * n), F32)], axis=0
        ).astype(BF16)
        if block in (1, 2):
            seen = seen_ref[:, (block - 1) * 8 * n : block * 8 * n]
        else:
            at = 0 if block == 0 else AT_JAC
            seen = jnp.concatenate(
                [halo[pl.ds(at + r, 128, stride=8), :] for r in range(8)], axis=1
            )
        resid = jnp.dot(resp_ref[...], model, preferred_element_type=F32) - seen
        weighted = jnp.clip(resid, -clip, clip)
        if first and block in (1, 2):
            loss = weighted * (resid - 0.5 * weighted)
            huber = huber + jnp.sum(loss.reshape(16, 8, 8 * n), axis=0)
        summed = jnp.dot(resp_t_ref[...], weighted.astype(BF16), preferred_element_type=F32)
        summed = split_rows(summed[:SPP] + summed[SPP:])
        for i in range(4):
            pair = 4 * block + i
            contracted[pair * HL : (pair + 1) * HL, :] = summed[:, 2 * n * i : 2 * n * (i + 1)]
    for block in range(2):
        windows = [
            contracted[(4 * block + k) * HL : (4 * block + k + 4) * HL, :] for k in range(PAIRS)
        ]
        back = jnp.dot(
            jnp.concatenate(windows, axis=1), adjoint_ref[...], preferred_element_type=F32
        )
        for i in range(4):
            pair = 4 * block + i
            both = back[i * HL : i * HL + SPP] + back[i * HL + SPP : (i + 1) * HL]
            along[pl.ds(2 * pair, SPP, stride=16), :] = both[:, :n]
            along[pl.ds(2 * pair + 1, SPP, stride=16), :] = both[:, n:]
    for p in range(9):
        total = jnp.zeros((16, n), F32)
        for s in range(4):
            image = s * 9 + p
            total = total + jac_ref[image].astype(F32) * along[image * 16 : image * 16 + 16, :]
        for copy in range(8):
            out_ref[copy, p * 16 : p * 16 + 16, :] = total
    loss = sum(huber[:, i * n : (i + 1) * n] for i in range(8))
    for copy in range(8):
        out_ref[copy, 144:152, :] = loss


def dual_kernel(step_ref, dual_step_ref, bound_ref, x_ref, dual_ref, lo_ref, hi_ref, dual_out_ref, moved_ref):
    n = LANES
    bound, dual_step = bound_ref[0], dual_step_ref[0]
    row = lax.broadcasted_iota(jnp.int32, (16, n), 0)
    duals = sum(lo_ref[AT_DUAL + 16 * i : AT_DUAL + 16 * i + 16, :].astype(F32) for i in range(3))
    for p in range(9):
        x = x_ref[p]
        after = halo_x(hi_ref, p)[0:1]
        before = halo_x(lo_ref, p)[15:16]
        grad_r = jnp.where(row == 15, after, pltpu.roll(x, 15, 0)) - x
        grad_c = pltpu.roll(x, n - 1, 1) - x
        dual_r = jnp.clip(dual_ref[0, p] + dual_step * grad_r, -bound, bound)
        dual_c = jnp.clip(dual_ref[1, p] + dual_step * grad_c, -bound, bound)
        prior = jnp.clip(duals[p : p + 1] + dual_step * (x[0:1] - before), -bound, bound)
        divergence = dual_r - jnp.where(row == 0, prior, pltpu.roll(dual_r, 1, 0))
        divergence = divergence + (dual_c - pltpu.roll(dual_c, 1, 1))
        dual_out_ref[0, p] = dual_r
        dual_out_ref[1, p] = dual_c
        moved_ref[p * 16 : p * 16 + 16, :] = step_ref[0] * divergence


def update_kernel(step_ref, whole_ref, x_ref, moved_ref, out_ref):
    total = sum(whole_ref[i] for i in range(8))
    out_ref[0:144, :] = x_ref[0:144, :] + moved_ref[...] - step_ref[0] * total[:144]
    out_ref[144:152, :] = total[144:]


def vmem_specs(count):
    return [pl.BlockSpec(memory_space=pltpu.VMEM) for _ in range(count)]


def smem_specs(count):
    return [pl.BlockSpec(memory_space=pltpu.SMEM) for _ in range(count)]


def call(kernel, shapes, scalars, arrays, name, scratch=(), flops=0):
    single = not isinstance(shapes, tuple)
    moved = sum(a.size * a.dtype.itemsize for a in arrays)
    return pl.pallas_call(
        kernel,
        out_shape=shapes,
        in_specs=smem_specs(len(scalars)) + vmem_specs(len(arrays)),
        out_specs=vmem_specs(1)[0] if single else tuple(vmem_specs(len(shapes))),
        scratch_shapes=list(scratch),
        compiler_params=pltpu.CompilerParams(vmem_limit_bytes=40 * 1024 * 1024),
        cost_estimate=pl.CostEstimate(flops=flops, bytes_accessed=moved, transcendentals=0),
        name=name,
    )(*[s.reshape(1) if s.ndim == 0 else s for s in scalars], *arrays)


def shaped(shape, dtype):
    return jax.ShapeDtypeStruct(shape, dtype)


def partial_gradient(first, clip_bound, halos, xs, jac, seen, resp, resp_t, forward, adjoint):
    return call(
        functools.partial(step_kernel, first),
        shaped((8, 152, LANES), F32),
        (clip_bound,),
        (*halos, *xs, jac, seen, resp, resp_t, forward, adjoint),
        "partial_gradient",
        (
            pltpu.VMEM((SPP * 48, LANES), F32),
            pltpu.VMEM((24 * HL, 2 * LANES), BF16),
            pltpu.VMEM((2 * AT_JAC, LANES), F32),
            pltpu.VMEM((16 * HL, 2 * LANES), BF16),
            pltpu.VMEM((SPP * 16, LANES), F32),
        ),
        flops=3_000_000_000,
    )


def response_matrices(response):
    block = jnp.einsum("st,pl->sltp", jnp.eye(4, dtype=F32), response).reshape(128, SP)
    block = jnp.pad(block, ((0, 0), (0, SPP - SP)))
    high = lax.reduce_precision(block, 8, 7)
    low = block - high
    forward = jnp.concatenate([high, high, low, jnp.zeros((128, 8), F32)], axis=1)
    backward = jnp.concatenate([high.T, low.T], axis=0)
    return forward.astype(BF16), backward.astype(BF16)


def per_device(
    params, dual_in, jacobian, response, observed, psf, step_size, dual_step, tv_bound, clip_bound
):
    stokes, waves, rows, ncol = observed.shape
    tiles, wavs = lax.axis_size(TILE), lax.axis_size(WAVE)
    jac = jacobian.reshape(SP, rows, ncol)
    obs = observed.reshape(stokes * waves, rows, ncol)
    flat = params.reshape(9 * rows, ncol)
    buffer = shaped((HALO, LANES), BF16)
    up, down = call(halo_kernel, (buffer, buffer), (), (params, dual_in, jac, obs), "halos")
    halos = (passed_along(up, 1), passed_along(down, -1))
    weights = shaped((18 * LANES, 2 * LANES), BF16)
    forward, adjoint, seen = call(
        weights_kernel,
        (weights, weights, shaped((stokes * waves, rows * ncol), F32)),
        (psf.astype(F32),),
        (obs,),
        "weights",
        (pltpu.VMEM((128 * 16, LANES), F32),),
        flops=5_000_000_000,
    )
    resp, resp_t = response_matrices(response)
    gradient = functools.partial(
        partial_gradient,
        clip_bound=clip_bound, halos=halos, jac=jac, seen=seen,
        resp=resp, resp_t=resp_t, forward=forward, adjoint=adjoint,
    )
    part = gradient(True, xs=(flat, flat, flat))
    whole = lax.all_to_all(part, WAVE, 0, 0, tiled=True)
    dual_out, moved = call(
        dual_kernel,
        (shaped((2, 9, rows, ncol), F32), shaped((9 * rows, ncol), F32)),
        (step_size, dual_step, tv_bound),
        (params, dual_in, *halos),
        "dual",
        flops=20_000_000,
    )
    updated = shaped((9 * rows + 8, ncol), F32)
    state = call(update_kernel, updated, (step_size,), (whole, flat, moved), "update")
    before, after = passed_along(state, 1), passed_along(state, -1)
    second = passed_along(state[9 * rows :], -2)
    loss = before[9 * rows :] + state[9 * rows :] + after[9 * rows :] + second
    each = tiles // wavs
    loss = lax.ppermute(
        loss,
        ALL,
        [
            (((t + each * w + 2) % tiles) * wavs + w, t * wavs + w)
            for t in range(tiles)
            for w in range(wavs)
        ],
    )
    part = gradient(False, xs=(before, state, after))
    part = part.at[:, 9 * rows :].set(loss)
    whole = lax.all_to_all(part, WAVE, 0, 0, tiled=True)
    state = call(update_kernel, updated, (step_size,), (whole, state, moved), "update")
    total = stokes * waves * wavs * rows * tiles * ncol
    misfit = jnp.sum(state[9 * rows :]) / total
    return (state[: 9 * rows].reshape(9, rows, ncol), dual_out, misfit)


def solution(mesh):
    split = Mesh(
        mesh.devices.reshape(2, 8, 2, 2, 4), ("tile_0", "tile_1", "tile_2", "wave_0", "wave_1")
    )
    placed = (
        P(None, TILE, None),
        P(None, None, TILE, None),
        P(None, None, TILE, None),
        P(None, WAVE),
        P(None, WAVE, TILE, None),
        P(),
        P(),
        P(),
        P(),
        P(),
    )
    return jax.shard_map(
        per_device,
        mesh=split,
        in_specs=placed,
        out_specs=(P(None, TILE, None), P(None, None, TILE, None), P()),
        check_vma=False,
    )
```
